32 devices in a mesh: dp: 4 (over y, core), tensor: 8 (over z, x).
Axes of the slice: x: 2, y: 2, z: 4, core: 2. Of those that a mesh axis runs over, the one named last changes fastest.
Arguments:
- block_input: float32 [4, 2048, 1024], P('dp', 'tensor'), may hold values from -6 to 6
- segment_ids: int32 [4, 2048], P('dp'), may hold values from 0 to 2, as said below
- positions: int32 [4, 2048], P('dp'), may hold values from 0 to 1791, as said below
- attention_gain: bfloat16 [1024], P('dp'), may hold values from 0.099609375 to 1.8984375
- feedforward_gain: bfloat16 [1024], P('dp'), may hold values from 0.099609375 to 1.8984375
- qkv_weight: bfloat16 [1024, 3, 1024], P('dp', None, 'tensor'), may hold values from -2 to 2, as said below
- output_weight: bfloat16 [1024, 1024], P('tensor', 'dp'), may hold values from -0.75 to 0.75
- expand_weight: bfloat16 [1024, 2, 2624], P('dp', None, 'tensor'), may hold values from -0.1875 to 0.1875
- contract_weight: bfloat16 [2624, 1024], P('tensor', 'dp'), may hold values from -0.25 to 0.25
- cotangent: float32 [4, 2048, 1024], P('dp', 'tensor'), may hold values from -6 to 6
Outputs:
- block_output: float32 [4, 2048, 1024], P('dp', 'tensor')
- input_grad: float32 [4, 2048, 1024], P('dp', 'tensor')
- attention_gain_grad: float32 [1024], P('dp')
- feedforward_gain_grad: float32 [1024], P('dp')
- qkv_grad: float32 [1024, 3, 1024], P('dp', None, 'tensor')
- output_grad: float32 [1024, 1024], P('tensor', 'dp')
- expand_grad: float32 [1024, 2, 2624], P('dp', None, 'tensor')
- contract_grad: float32 [2624, 1024], P('tensor', 'dp')
The draws below stay inside these ranges and needn't reach their ends.
Inputs may be any that keep to these rules, and one draw needn't show every extreme that they name: `segment_ids`: within each sequence the numbers never fall; a token's number tells its document, and a number may be skipped. `positions`: each token's position counts the tokens before it in its own document; no document is longer than 1792 tokens, and some document is that long. `qkv_weight`: the joined query, key and value projection.
All inputs are finite; a program needn't handle non-finite values.
Results may differ from the reference program's by a relative error of at most 0.025.
Values may be sent and summed in bfloat16 or wider, within the bound.
A program may use at most 128 MiB of HBM per device.

```python
import math
import jax
import jax.numpy as jnp
from jax import lax

D = 1024
H = 16
HD = 64
FF = 2624
WINDOW = 128
L = 2048
SEQS = 4


def document_cuts(key):
    lowest = L // 8
    first_cut = jax.random.randint(jax.random.fold_in(key, 11), (SEQS, 1), lowest, L - lowest + 1)
    second_cut = jax.random.randint(jax.random.fold_in(key, 12), (SEQS, 1), lowest, L - lowest + 1)
    leading = jnp.arange(SEQS, dtype=jnp.int32)[:, None] == 0
    first_cut = jnp.where(leading, L - lowest, first_cut).astype(jnp.int32)
    second_cut = jnp.where(leading, L - lowest, second_cut).astype(jnp.int32)
    index_row = jnp.arange(L, dtype=jnp.int32)[None, :]
    return (first_cut, second_cut, index_row)


def draw_segment_ids(key, part):
    first_cut, second_cut, index_row = document_cuts(key)
    return (index_row >= first_cut).astype(jnp.int32) + (index_row >= second_cut).astype(jnp.int32)


def draw_positions(key, part):
    first_cut, second_cut, index_row = document_cuts(key)
    begins = jnp.maximum(jnp.where(index_row >= first_cut, first_cut, 0), jnp.where(index_row >= second_cut, second_cut, 0))
    return (index_row - begins).astype(jnp.int32)


def draw_qkv_weight(key, part):
    base = jax.random.normal(jax.random.fold_in(key, 21), (D, 3, D), jnp.float32)
    return (base * D ** (-0.5)).astype(jnp.bfloat16)


def block_scale(own_key, dims, cuts, low, high):
    factor_of = 1.0
    for axis_at, blocks in cuts:
        heights = jax.random.uniform(jax.random.fold_in(jax.random.fold_in(own_key, 6), axis_at), (blocks,), jnp.float32, low / len(cuts), high / len(cuts))
        factor_of = factor_of * jnp.repeat(jnp.exp(heights), dims[axis_at] // blocks).reshape((-1,) + (1,) * (len(dims) - 1 - axis_at))
    return factor_of


def centred(key, extent, spread, bound, cuts=(), kind=jnp.bfloat16):
    values = jax.random.normal(key, extent, jnp.float32) * spread
    if len(cuts) > 0:
        values = block_scale(key, extent, cuts, -0.22, 0.18) * values
    return jnp.clip(values, min=-bound, max=bound).astype(kind)


def setup_inputs(seed: int = 0) -> dict:
    key_of = jax.random.split(jax.random.key(seed), 11)
    block_input = centred(key_of[0], (SEQS, L, D), 1.0, 6.0, ((0, 4), (1, 8)), jnp.float32)
    segment_ids = draw_segment_ids(jax.random.fold_in(key_of[10], 71), 0)
    positions = draw_positions(jax.random.fold_in(key_of[10], 71), 0)
    attention_gain = jnp.clip(1.0 + 0.18 * jax.random.normal(key_of[3], (D,), jnp.float32), 0.099609375, 1.8984375).astype(jnp.bfloat16)
    feedforward_gain = jnp.clip(1.0 + 0.18 * jax.random.normal(key_of[4], (D,), jnp.float32), 0.099609375, 1.8984375).astype(jnp.bfloat16)
    qkv_weight = draw_qkv_weight(jax.random.fold_in(key_of[10], 71), 0)
    output_weight = centred(key_of[6], (D, D), (D // 16) ** -0.5, 0.75, ((0, 8), (1, 4)))
    expand_weight = centred(key_of[7], (D, 2, FF), D ** -0.5, 0.1875, ((0, 4), (2, 8)))
    contract_weight = centred(key_of[8], (FF, D), (FF // 4) ** -0.5, 0.25, ((0, 8), (1, 4)))
    cotangent = centred(key_of[9], (SEQS, L, D), 1.0, 6.0, ((0, 4), (1, 8)), jnp.float32)
    return {"block_input": block_input, "segment_ids": segment_ids, "positions": positions, "attention_gain": attention_gain, "feedforward_gain": feedforward_gain, "qkv_weight": qkv_weight, "output_weight": output_weight, "expand_weight": expand_weight, "contract_weight": contract_weight, "cotangent": cotangent}


EPSILON = 1e-05
MASKED = -1e+30
ROOT_HALF = 0.7071067811865476
DENSITY = 0.3989422804014327

def widen(tensor):
    return lax.optimization_barrier(tensor).astype(jnp.float32)

def layer_norm(values, gain_vector):
    centre = values - lax.optimization_barrier(jnp.mean(values, axis=-1, keepdims=True))
    variance = lax.optimization_barrier(jnp.mean(centre * centre, axis=-1, keepdims=True))
    inverse = lax.rsqrt(variance + EPSILON)
    normed = centre * inverse
    return (normed, inverse, (normed * gain_vector.astype(jnp.float32)).astype(jnp.bfloat16))

def norm_backward(upstream, normed, inverse, gain_vector):
    scaled = upstream * gain_vector.astype(jnp.float32)
    inner_term = scaled - lax.optimization_barrier(jnp.mean(scaled, axis=-1, keepdims=True)) - normed * lax.optimization_barrier(jnp.mean(scaled * normed, axis=-1, keepdims=True))
    return (inverse * inner_term, lax.optimization_barrier(jnp.sum(upstream * normed, axis=0)))

def gelu_pair(values):
    normal_cdf = 0.5 * (1.0 + lax.erf(values * ROOT_HALF))
    return (values * normal_cdf, normal_cdf + values * DENSITY * jnp.exp(-0.5 * values * values))

def rope_tables(places, head_size):
    half_size = head_size // 2
    frequency = jnp.exp(jnp.arange(half_size, dtype=jnp.float32) * (-2.0 * math.log(10000.0) / head_size))
    angles = places.astype(jnp.float32)[:, None] * frequency[None, :]
    cosine_table = jnp.concatenate([jnp.cos(angles), jnp.cos(angles)], axis=-1)[:, None, :]
    sine_table = jnp.concatenate([jnp.sin(angles), jnp.sin(angles)], axis=-1)[:, None, :]
    return (cosine_table, sine_table)

def rotate(tensor, cosine_table, sine_table):
    half_size = tensor.shape[-1] // 2
    turned = jnp.concatenate([-tensor[..., half_size:], tensor[..., :half_size]], axis=-1)
    return tensor * cosine_table + turned * sine_table

def unrotate(tensor, cosine_table, sine_table):
    half_size = tensor.shape[-1] // 2
    weighted = tensor * sine_table
    turned = jnp.concatenate([weighted[..., half_size:], -weighted[..., :half_size]], axis=-1)
    return tensor * cosine_table + turned

def block_scores(query_block, key_block, segment_query, segment_key, block_rows, scale):
    reach = WINDOW // 2
    scores = jnp.einsum('qhd,khd->hqk', widen(query_block), widen(key_block)) * scale
    offset = jnp.arange(block_rows)[:, None] + reach - jnp.arange(block_rows + 2 * reach)[None, :]
    valid = (jnp.abs(offset) <= reach) & (segment_query[:, None] == segment_key[None, :])
    return jnp.where(valid[None], scores, MASKED)

def band_pads(keys, values, segments):
    reach = WINDOW // 2
    pad_keys = jnp.pad(keys, ((reach, reach), (0, 0), (0, 0)))
    pad_values = jnp.pad(values, ((reach, reach), (0, 0), (0, 0)))
    pad_segments = jnp.pad(segments, (reach, reach), constant_values=-1)
    return (pad_keys, pad_values, pad_segments)

def band_forward(queries, keys, values, segments):
    length, heads, head_size = queries.shape
    reach = WINDOW // 2
    block = min(length, 512)
    scale = head_size ** (-0.5)
    pad_keys, pad_values, pad_segments = band_pads(keys, values, segments)

    def one_block(index):
        start = (index * block).astype(jnp.int32)
        query_block = lax.dynamic_slice_in_dim(queries, start, block, 0)
        key_block = lax.dynamic_slice_in_dim(pad_keys, start, block + 2 * reach, 0)
        value_block = lax.dynamic_slice_in_dim(pad_values, start, block + 2 * reach, 0)
        segment_query = lax.dynamic_slice_in_dim(segments, start, block, 0)
        segment_key = lax.dynamic_slice_in_dim(pad_segments, start, block + 2 * reach, 0)
        scores = block_scores(query_block, key_block, segment_query, segment_key, block, scale)
        peak = lax.optimization_barrier(jnp.max(scores, axis=-1, keepdims=True))
        log_total = peak + jnp.log(lax.optimization_barrier(jnp.sum(jnp.exp(scores - peak), axis=-1, keepdims=True)))
        weights = jnp.exp(scores - log_total).astype(jnp.bfloat16)
        context = jnp.einsum('hqk,khd->qhd', widen(weights), widen(value_block)).astype(jnp.bfloat16)
        return (context, log_total[..., 0])
    contexts, totals = lax.map(one_block, jnp.arange(length // block, dtype=jnp.int32))
    return (contexts.reshape(length, heads, head_size), totals)

def band_backward(queries, keys, values, segments, grad_context, totals):
    length, heads, head_size = queries.shape
    reach = WINDOW // 2
    block = min(length, 512)
    span = block + 2 * reach
    scale = head_size ** (-0.5)
    pad_keys, pad_values, pad_segments = band_pads(keys, values, segments)

    def one_block(carry, index):
        grad_keys, grad_values = carry
        start = (index * block).astype(jnp.int32)
        query_block = lax.dynamic_slice_in_dim(queries, start, block, 0)
        key_block = lax.dynamic_slice_in_dim(pad_keys, start, span, 0)
        value_block = lax.dynamic_slice_in_dim(pad_values, start, span, 0)
        segment_query = lax.dynamic_slice_in_dim(segments, start, block, 0)
        segment_key = lax.dynamic_slice_in_dim(pad_segments, start, span, 0)
        grad_block = lax.dynamic_slice_in_dim(grad_context, start, block, 0)
        scores = block_scores(query_block, key_block, segment_query, segment_key, block, scale)
        probs = jnp.exp(scores - totals[index][..., None])
        grad_probs = jnp.einsum('qhd,khd->hqk', widen(grad_block), widen(value_block))
        delta = lax.optimization_barrier(jnp.sum(probs * grad_probs, axis=-1, keepdims=True))
        grad_scores = (probs * (grad_probs - delta) * scale).astype(jnp.bfloat16)
        grad_query = jnp.einsum('hqk,khd->qhd', widen(grad_scores), widen(key_block))
        key_part = jnp.einsum('hqk,qhd->khd', widen(grad_scores), widen(query_block))
        value_part = jnp.einsum('hqk,qhd->khd', widen(probs.astype(jnp.bfloat16)), widen(grad_block))
        grad_keys = lax.dynamic_update_slice_in_dim(grad_keys, lax.dynamic_slice_in_dim(grad_keys, start, span, 0) + key_part, start, 0)
        grad_values = lax.dynamic_update_slice_in_dim(grad_values, lax.dynamic_slice_in_dim(grad_values, start, span, 0) + value_part, start, 0)
        return ((grad_keys, grad_values), grad_query)
    zeros = jnp.zeros((length + 2 * reach, heads, head_size), jnp.float32)
    (grad_keys, grad_values), grad_queries = lax.scan(one_block, (zeros, zeros), jnp.arange(length // block, dtype=jnp.int32))
    return (grad_queries.reshape(length, heads, head_size), grad_keys[reach:reach + length], grad_values[reach:reach + length])

def reference(block_input, segment_ids, positions, attention_gain, feedforward_gain, qkv_weight, output_weight, expand_weight, contract_weight, cotangent):
    qkv_matrix = qkv_weight.reshape(D, 3 * D)
    expand_matrix = expand_weight.reshape(D, 2 * FF)

    def sequence_pass(carry, items):
        grad_qkv, grad_output, grad_expand, grad_contract, gain_first, gain_second = carry
        tokens, segments, places, upstream = items
        cosine_table, sine_table = rope_tables(places, HD)
        normed_one, inverse_one, rows_one = layer_norm(tokens, attention_gain)
        projected = jnp.dot(rows_one, qkv_matrix, preferred_element_type=jnp.float32).reshape(L, 3, H, HD)
        queries = rotate(projected[:, 0], cosine_table, sine_table).astype(jnp.bfloat16)
        keys = rotate(projected[:, 1], cosine_table, sine_table).astype(jnp.bfloat16)
        values_in = projected[:, 2].astype(jnp.bfloat16)
        context, totals = band_forward(queries, keys, values_in, segments)
        context_rows = context.reshape(L, D)
        residual = tokens + jnp.dot(context_rows, output_weight, preferred_element_type=jnp.float32)
        normed_two, inverse_two, rows_two = layer_norm(residual, feedforward_gain)
        expanded = jnp.dot(rows_two, expand_matrix, preferred_element_type=jnp.float32).reshape(L, 2, FF)
        activated, slope = gelu_pair(expanded[:, 0])
        hidden = (activated * expanded[:, 1]).astype(jnp.bfloat16)
        result = residual + jnp.dot(hidden, contract_weight, preferred_element_type=jnp.float32)
        rows_back = upstream.astype(jnp.bfloat16)
        grad_contract = grad_contract + jnp.dot(hidden.T, rows_back, preferred_element_type=jnp.float32)
        grad_hidden = jnp.dot(rows_back, contract_weight.T, preferred_element_type=jnp.float32)
        grad_units = jnp.stack([grad_hidden * expanded[:, 1] * slope, grad_hidden * activated], axis=1).astype(jnp.bfloat16).reshape(L, 2 * FF)
        grad_expand = grad_expand + jnp.dot(rows_two.T, grad_units, preferred_element_type=jnp.float32)
        grad_two = jnp.dot(grad_units, expand_matrix.T, preferred_element_type=jnp.float32)
        through_two, gain_part = norm_backward(grad_two, normed_two, inverse_two, feedforward_gain)
        gain_second = gain_second + gain_part
        grad_mid = upstream + through_two
        rows_mid = grad_mid.astype(jnp.bfloat16)
        grad_output = grad_output + jnp.dot(context_rows.T, rows_mid, preferred_element_type=jnp.float32)
        grad_context = jnp.dot(rows_mid, output_weight.T, preferred_element_type=jnp.float32).astype(jnp.bfloat16).reshape(L, H, HD)
        grad_queries, grad_keys, grad_values = band_backward(queries, keys, values_in, segments, grad_context, totals)
        grad_proj = jnp.stack([unrotate(grad_queries, cosine_table, sine_table), unrotate(grad_keys, cosine_table, sine_table), grad_values], axis=1).astype(jnp.bfloat16).reshape(L, 3 * D)
        grad_qkv = grad_qkv + jnp.dot(rows_one.T, grad_proj, preferred_element_type=jnp.float32)
        grad_one = jnp.dot(grad_proj, qkv_matrix.T, preferred_element_type=jnp.float32)
        through_one, gain_part = norm_backward(grad_one, normed_one, inverse_one, attention_gain)
        gain_first = gain_first + gain_part
        return ((grad_qkv, grad_output, grad_expand, grad_contract, gain_first, gain_second), (result, grad_mid + through_one))
    start_carry = (jnp.zeros((D, 3 * D), jnp.float32), jnp.zeros((D, D), jnp.float32), jnp.zeros((D, 2 * FF), jnp.float32), jnp.zeros((FF, D), jnp.float32), jnp.zeros((D,), jnp.float32), jnp.zeros((D,), jnp.float32))
    final, stacked = lax.scan(sequence_pass, start_carry, (block_input, segment_ids, positions, cotangent))
    grad_qkv, grad_output, grad_expand, grad_contract, gain_first, gain_second = final
    return (stacked[0], stacked[1], gain_first, gain_second, grad_qkv.reshape(D, 3, D), grad_output, grad_expand.reshape(D, 2, FF), grad_contract)
```

```python
import functools
import math

import jax
import jax.numpy as jnp
from jax import lax
from jax.experimental import pallas as pl
from jax.experimental.pallas import tpu as pltpu
from jax.sharding import PartitionSpec as P

HD = 64
WINDOW = 128
REACH = WINDOW // 2
EPSILON = 1e-05
MASKED = -1e30
ROOT_HALF = 0.7071067811865476
DENSITY = 0.3989422804014327
BOTH = ("dp", "tensor")
GAIN_ROWS = 16
CHUNKS = 2
NN = (((1,), (0,)), ((), ()))
NT = (((1,), (1,)), ((), ()))
TN = (((0,), (0,)), ((), ()))


def mm(left, right, dims):
    return lax.dot_general(left, right, dims, preferred_element_type=jnp.float32)


def norm_rows(values):
    centre = values - jnp.mean(values, axis=-1, keepdims=True)
    variance = jnp.mean(centre * centre, axis=-1, keepdims=True)
    inverse = lax.rsqrt(variance + EPSILON)
    return centre * inverse, inverse


def norm_back(upstream, normed, inverse, gain):
    scaled = upstream * gain
    inner = (
        scaled
        - jnp.mean(scaled, axis=-1, keepdims=True)
        - normed * jnp.mean(scaled * normed, axis=-1, keepdims=True)
    )
    return inverse * inner


def wide(ref, part):
    return jnp.concatenate([ref[d, 0, part] for d in range(ref.shape[0])], axis=1)


def spread(ref, part, value):
    rows = ref.shape[-1]
    for d in range(ref.shape[0]):
        ref[d, 0, part] = value[:, d * rows : (d + 1) * rows].astype(ref.dtype)


def turn(tensor, first_sign):
    half = HD // 2
    pieces = []
    for head in range(tensor.shape[1] // HD):
        low = tensor[:, head * HD : head * HD + half]
        high = tensor[:, head * HD + half : (head + 1) * HD]
        pieces += [-high, low] if first_sign < 0 else [high, -low]
    return jnp.concatenate(pieces, axis=1)


def blocks_of(tokens):
    size = min(tokens, 128)
    return [(start, size, size + 2 * REACH) for start in range(0, tokens, size)]


def band_mask(segq, segk, start, size, span):
    rows = lax.broadcasted_iota(jnp.int32, (size, span), 0)
    cols = lax.broadcasted_iota(jnp.int32, (size, span), 1)
    near = jnp.abs(rows + REACH - cols) <= REACH
    return near & (segq[start : start + size, :] == segk[:, start : start + span])


def attend_kernel(x_ref, gain_ref, w_ref, cos_ref, sin_ref, segq_ref, segk_ref,
                  y_ref, qkv_ref, ctx_ref, lse_ref, a_ref):
    step = pl.program_id(0)
    tokens = y_ref.shape[0]
    scale = HD ** (-0.5)

    @pl.when(step == 0)
    def _():
        normed, _ = norm_rows(x_ref[...])
        a_ref[...] = (normed * gain_ref[...].astype(jnp.float32)).astype(jnp.bfloat16)
        y_ref[...] = x_ref[REACH : REACH + tokens, :]

    a = a_ref[...]
    cos, sin = cos_ref[...], sin_ref[...]
    q = mm(a, wide(w_ref, 0), NT)
    k = mm(a, wide(w_ref, 1), NT)
    v = mm(a, wide(w_ref, 2), NT).astype(jnp.bfloat16)
    q = (q * cos + turn(q, -1) * sin).astype(jnp.bfloat16)
    k = (k * cos + turn(k, -1) * sin).astype(jnp.bfloat16)
    qkv_ref[0, 0], qkv_ref[0, 1], qkv_ref[0, 2] = q, k, v
    heads = q.shape[1] // HD
    segq, segk = segq_ref[...], segk_ref[...]
    contexts, totals = [], []
    for start, size, span in blocks_of(tokens):
        valid = band_mask(segq, segk, start, size, span)
        row_ctx, row_lse = [], []
        for head in range(heads):
            lanes = slice(head * HD, (head + 1) * HD)
            qb = q[REACH + start : REACH + start + size, lanes]
            kb = k[start : start + span, lanes]
            vb = v[start : start + span, lanes]
            s = jnp.where(valid, mm(qb, kb, NT) * scale, MASKED)
            peak = jnp.max(s, axis=-1, keepdims=True)
            total = peak + jnp.log(jnp.sum(jnp.exp(s - peak), axis=-1, keepdims=True))
            weights = jnp.exp(s - total).astype(jnp.bfloat16)
            row_ctx.append(mm(weights, vb, NN))
            row_lse.append(total)
        contexts.append(jnp.concatenate(row_ctx, axis=1))
        totals.append(jnp.concatenate(row_lse, axis=1))
    context = jnp.concatenate(contexts, axis=0).astype(jnp.bfloat16)
    ctx_ref[0] = context
    lse_ref[0] = jnp.concatenate(totals, axis=0)
    y_ref[...] += mm(context, wide(w_ref, 3), NN)


def attend_back_kernel(x_ref, gain_ref, w_ref, cos_ref, sin_ref, segq_ref, segk_ref,
                       qkv_ref, ctx_ref, lse_ref, dy_ref,
                       dw_ref, da_ref, gg_ref, a_ref, n_ref, d_ref):
    step = pl.program_id(0)
    tokens = dy_ref.shape[0]
    scale = HD ** (-0.5)

    @pl.when(step == 0)
    def _():
        normed, _ = norm_rows(x_ref[...])
        n_ref[...] = normed
        a_ref[...] = (normed * gain_ref[...].astype(jnp.float32)).astype(jnp.bfloat16)
        d_ref[...] = dy_ref[...].astype(jnp.bfloat16)
        da_ref[...] = jnp.zeros_like(da_ref)

    dyb = d_ref[...]
    dc = mm(dyb, wide(w_ref, 3), NT).astype(jnp.bfloat16)
    spread(dw_ref, 3, mm(ctx_ref[0], dyb, TN))
    q, k, v = qkv_ref[0, 0], qkv_ref[0, 1], qkv_ref[0, 2]
    heads = q.shape[1] // HD
    segq, segk = segq_ref[...], segk_ref[...]
    lse = lse_ref[0]
    extent = tokens + 2 * REACH
    width = q.shape[1]
    dq_rows = []
    dk = jnp.zeros((extent, width), jnp.float32)
    dv = jnp.zeros((extent, width), jnp.float32)
    for start, size, span in blocks_of(tokens):
        valid = band_mask(segq, segk, start, size, span)
        dq_parts, dk_parts, dv_parts = [], [], []
        for head in range(heads):
            lanes = slice(head * HD, (head + 1) * HD)
            qb = q[REACH + start : REACH + start + size, lanes]
            kb = k[start : start + span, lanes]
            vb = v[start : start + span, lanes]
            db = dc[start : start + size, lanes]
            s = jnp.where(valid, mm(qb, kb, NT) * scale, MASKED)
            probs = jnp.exp(s - lse[start : start + size, head : head + 1])
            dp = mm(db, vb, NT)
            delta = jnp.sum(probs * dp, axis=-1, keepdims=True)
            ds = (probs * (dp - delta) * scale).astype(jnp.bfloat16)
            dq_parts.append(mm(ds, kb, NN))
            dk_parts.append(mm(ds, qb, TN))
            dv_parts.append(mm(probs.astype(jnp.bfloat16), db, TN))
        dq_rows.append(jnp.concatenate(dq_parts, axis=1))
        pads = ((start, extent - start - span), (0, 0))
        for parts, which in ((dk_parts, 0), (dv_parts, 1)):
            block = jnp.concatenate(parts, axis=1)
            rows = []
            if pads[0][0]:
                rows.append(jnp.zeros((pads[0][0], width), jnp.float32))
            rows.append(block)
            if pads[0][1]:
                rows.append(jnp.zeros((pads[0][1], width), jnp.float32))
            block = jnp.concatenate(rows, axis=0) if len(rows) > 1 else block
            if which == 0:
                dk = dk + block
            else:
                dv = dv + block
    cos, sin = cos_ref[...], sin_ref[...]
    dq = jnp.concatenate(dq_rows, axis=0)
    inner = slice(REACH, REACH + tokens)
    dq = (dq * cos[inner] + turn(dq * sin[inner], 1)).astype(jnp.bfloat16)
    dk = (dk * cos + turn(dk * sin, 1)).astype(jnp.bfloat16)
    dv = dv.astype(jnp.bfloat16)
    a = a_ref[...]
    spread(dw_ref, 0, mm(dq, a[inner], TN))
    spread(dw_ref, 1, mm(dk, a, TN))
    spread(dw_ref, 2, mm(dv, a, TN))
    da_ref[...] += mm(dk, wide(w_ref, 1), NN) + mm(dv, wide(w_ref, 2), NN)
    da_ref[inner, :] += mm(dq, wide(w_ref, 0), NN)

    @pl.when(step == pl.num_programs(0) - 1)
    def _():
        gg_ref[...] = jnp.sum(da_ref[...] * n_ref[...], axis=0, keepdims=True)


def feed_kernel(y_ref, gain_ref, up_ref, w_ref, out0_ref, da0_ref,
                dw_ref, out_ref, da_ref, a_ref, u_ref):
    step = pl.program_id(0)

    @pl.when(step == 0)
    def _():
        normed, _ = norm_rows(y_ref[...])
        a_ref[...] = (normed * gain_ref[...].astype(jnp.float32)).astype(jnp.bfloat16)
        u_ref[...] = up_ref[...].astype(jnp.bfloat16)
        out_ref[...] = out0_ref[...]
        da_ref[...] = da0_ref[...]

    a, up = a_ref[...], u_ref[...]
    w0, w1, c = wide(w_ref, 0), wide(w_ref, 1), wide(w_ref, 2)
    u0 = mm(w0, a, NT)
    u1 = mm(w1, a, NT)
    cdf = 0.5 * (1.0 + lax.erf(u0 * ROOT_HALF))
    activated = u0 * cdf
    slope = cdf + u0 * DENSITY * jnp.exp(-0.5 * u0 * u0)
    hidden = (activated * u1).astype(jnp.bfloat16)
    out_ref[...] += mm(hidden, c, TN)
    spread(dw_ref, 2, mm(hidden, up, NN))
    dg = mm(c, up, NT)
    du0 = (dg * u1 * slope).astype(jnp.bfloat16)
    du1 = (dg * activated).astype(jnp.bfloat16)
    spread(dw_ref, 0, mm(du0, a, NN))
    spread(dw_ref, 1, mm(du1, a, NN))
    da_ref[...] += mm(du0, w0, TN) + mm(du1, w1, TN)


def full_spec(shape):
    return pl.BlockSpec(shape, lambda t: (0,) * len(shape))


def weight_spec(shape):
    return pl.BlockSpec(
        (shape[0], 1) + shape[2:], lambda t: (0, t) + (0,) * (len(shape) - 2)
    )


def lead_spec(shape):
    return pl.BlockSpec((1,) + shape[1:], lambda t: (t,) + (0,) * (len(shape) - 1))


def params():
    return pltpu.CompilerParams(
        dimension_semantics=("arbitrary",), vmem_limit_bytes=56 * 1024 * 1024
    )


def shaped(shape, dtype):
    return jax.ShapeDtypeStruct(shape, dtype)


def cost(flops, moved):
    return pl.CostEstimate(flops=int(flops), bytes_accessed=int(moved), transcendentals=0)


def body(
    dps,
    tensors,
    block_input,
    segment_ids,
    positions,
    attention_gain,
    feedforward_gain,
    qkv_weight,
    output_weight,
    expand_weight,
    contract_weight,
    cotangent,
):
    tokens, width = block_input.shape[1:]
    rows = qkv_weight.shape[0]
    hw = qkv_weight.shape[2]
    units = contract_weight.shape[0]
    heads = hw // HD
    extent = tokens + 2 * REACH
    f32, bf16 = jnp.float32, jnp.bfloat16

    x = block_input[0]
    upstream = cotangent[0]
    place = lax.axis_index("tensor")
    ahead = [(i, i + 1) for i in range(tensors - 1)]
    behind = [(i + 1, i) for i in range(tensors - 1)]
    before = lax.ppermute(x[tokens - REACH :], "tensor", ahead)
    after = lax.ppermute(x[:REACH], "tensor", behind)
    x_ext = jnp.concatenate([before, x, after], axis=0)

    gains = jnp.stack([attention_gain, feedforward_gain])
    first = jnp.concatenate(
        [
            jnp.transpose(qkv_weight, (1, 2, 0)).reshape(3 * hw, rows),
            output_weight,
            jnp.pad(gains, ((0, GAIN_ROWS - 2), (0, 0))),
        ],
        axis=0,
    )
    got_first = lax.all_gather(first, BOTH, axis=0, tiled=False).reshape(
        dps, tensors, 4 * hw + GAIN_ROWS, rows
    )
    stacked = jnp.concatenate(
        [jnp.transpose(expand_weight, (1, 2, 0)), contract_weight[None]], axis=0
    )
    cut = -(-units // (8 * CHUNKS)) * 8
    edges = [min(i * cut, units) for i in range(CHUNKS + 1)]
    got_feed = [
        lax.all_gather(stacked[:, lo:hi], BOTH, axis=0, tiled=False).reshape(
            dps, tensors, 3, hi - lo, rows
        )
        for lo, hi in zip(edges[:-1], edges[1:])
    ]
    gain_rows = got_first[:, 0, 4 * hw : 4 * hw + 2]
    gain_one = gain_rows[:, 0].reshape(1, width)
    gain_two = gain_rows[:, 1].reshape(1, width)
    w_attn = got_first[:, :, : 4 * hw].reshape(dps, tensors, 4, hw, rows)

    seg_all = jnp.pad(segment_ids[0], (REACH, REACH), constant_values=-1)
    pos_all = jnp.pad(positions[0], (REACH, REACH))
    seg_k = lax.dynamic_slice_in_dim(seg_all, place * tokens, extent, 0)
    pos = lax.dynamic_slice_in_dim(pos_all, place * tokens, extent, 0)
    seg_q = seg_k[REACH : REACH + tokens]
    half = HD // 2
    frequency = jnp.exp(jnp.arange(half, dtype=f32) * (-2.0 * math.log(10000.0) / HD))
    angles = pos.astype(f32)[:, None] * frequency[None, :]
    cos = jnp.tile(jnp.cos(angles), (1, 2 * heads))
    sin = jnp.tile(jnp.sin(angles), (1, 2 * heads))
    seg_q, seg_k = seg_q[:, None], seg_k[None, :]

    w_shape = w_attn.shape
    side = [
        full_spec((extent, width)),
        full_spec((1, width)),
        weight_spec(w_shape),
        full_spec((extent, hw)),
        full_spec((extent, hw)),
        full_spec((tokens, 1)),
        full_spec((1, extent)),
    ]
    qkv_shape = (tensors, 3, extent, hw)
    ctx_shape = (tensors, tokens, hw)
    lse_shape = (tensors, tokens, heads)
    attn_flops = 2 * tensors * extent * 4 * hw * width
    attn_bytes = 2 * 4 * width * width
    y, qkv, ctx, lse = pl.pallas_call(
        attend_kernel,
        grid=(tensors,),
        in_specs=side,
        out_specs=[
            full_spec((tokens, width)),
            lead_spec(qkv_shape),
            lead_spec(ctx_shape),
            lead_spec(lse_shape),
        ],
        out_shape=[
            shaped((tokens, width), f32),
            shaped(qkv_shape, bf16),
            shaped(ctx_shape, bf16),
            shaped(lse_shape, f32),
        ],
        scratch_shapes=[pltpu.VMEM((extent, width), bf16)],
        compiler_params=params(),
        cost_estimate=cost(attn_flops, attn_bytes),
        name="attend",
    )(x_ext, gain_one, w_attn, cos, sin, seg_q, seg_k)

    out, da_two = y, jnp.zeros((tokens, width), f32)
    owned_feed = []
    for got in got_feed:
        size = got.shape[3]
        dw, out, da_two = pl.pallas_call(
            feed_kernel,
            grid=(tensors,),
            in_specs=[
                full_spec((tokens, width)),
                full_spec((1, width)),
                full_spec((tokens, width)),
                weight_spec(got.shape),
                full_spec((tokens, width)),
                full_spec((tokens, width)),
            ],
            out_specs=[
                weight_spec(got.shape),
                full_spec((tokens, width)),
                full_spec((tokens, width)),
            ],
            out_shape=[
                shaped(got.shape, bf16),
                shaped((tokens, width), f32),
                shaped((tokens, width), f32),
            ],
            scratch_shapes=[
                pltpu.VMEM((tokens, width), bf16),
                pltpu.VMEM((tokens, width), bf16),
            ],
            compiler_params=params(),
            cost_estimate=cost(18 * tensors * tokens * size * width, 12 * tensors * size * width),
            name="feed",
        )(y, gain_two, upstream, got, out, da_two)
        owned_feed.append(
            lax.psum_scatter(
                dw.reshape((dps * tensors,) + got.shape[2:]),
                BOTH,
                scatter_dimension=0,
                tiled=True,
            )[0]
        )

    normed_two, inverse_two = norm_rows(y)
    gain_grad_two = jnp.sum(da_two * normed_two, axis=0)
    grad_mid = upstream + norm_back(da_two, normed_two, inverse_two, gain_two.astype(f32))

    dw_shape = (dps, tensors, 4 * hw + GAIN_ROWS, rows)
    dw_view = (dps, tensors, 4, hw, rows)
    dw_attn, da_one, gain_grad_one = pl.pallas_call(
        attend_back_kernel,
        grid=(tensors,),
        in_specs=side
        + [
            lead_spec(qkv_shape),
            lead_spec(ctx_shape),
            lead_spec(lse_shape),
            full_spec((tokens, width)),
        ],
        out_specs=[
            weight_spec(dw_view),
            full_spec((extent, width)),
            full_spec((1, width)),
        ],
        out_shape=[
            shaped(dw_view, bf16),
            shaped((extent, width), f32),
            shaped((1, width), f32),
        ],
        scratch_shapes=[
            pltpu.VMEM((extent, width), bf16),
            pltpu.VMEM((extent, width), f32),
            pltpu.VMEM((tokens, width), bf16),
        ],
        compiler_params=params(),
        cost_estimate=cost(2 * attn_flops, 2 * attn_bytes),
        name="attend_back",
    )(x_ext, gain_one, w_attn, cos, sin, seg_q, seg_k, qkv, ctx, lse, grad_mid)

    gain_grads = jnp.stack([gain_grad_one[0], gain_grad_two]).reshape(2, dps, rows)
    gain_block = jnp.broadcast_to(
        jnp.pad(jnp.transpose(gain_grads, (1, 0, 2)), ((0, 0), (0, GAIN_ROWS - 2), (0, 0)))[
            :, None
        ],
        (dps, tensors, GAIN_ROWS, rows),
    ).astype(bf16)
    last = jnp.concatenate(
        [dw_attn.reshape(dps, tensors, 4 * hw, rows), gain_block], axis=2
    ).reshape((dps * tensors,) + dw_shape[2:])
    owned = lax.psum_scatter(last, BOTH, scatter_dimension=0, tiled=True)[0]

    to_before = lax.ppermute(da_one[:REACH].astype(bf16), "tensor", behind).astype(f32)
    to_after = lax.ppermute(da_one[tokens + REACH :].astype(bf16), "tensor", ahead).astype(f32)
    da_total = da_one[REACH : REACH + tokens]
    da_total = da_total + jnp.concatenate(
        [to_after, jnp.zeros((tokens - 2 * REACH, width), f32), to_before], axis=0
    )
    normed_one, inverse_one = norm_rows(x)
    input_grad = grad_mid + norm_back(da_total, normed_one, inverse_one, gain_one.astype(f32))

    feed = jnp.concatenate(owned_feed, axis=1)
    return (
        out[None],
        input_grad[None],
        owned[4 * hw].astype(f32),
        owned[4 * hw + 1].astype(f32),
        jnp.transpose(owned[: 3 * hw].reshape(3, hw, rows), (2, 0, 1)).astype(f32),
        owned[3 * hw : 4 * hw].astype(f32),
        jnp.transpose(feed[:2], (2, 0, 1)).astype(f32),
        feed[2].astype(f32),
    )


def solution(mesh):
    return jax.shard_map(
        functools.partial(body, mesh.shape["dp"], mesh.shape["tensor"]),
        mesh=mesh,
        in_specs=(
            P("dp", "tensor", None),
            P("dp", None),
            P("dp", None),
            P("dp"),
            P("dp"),
            P("dp", None, "tensor"),
            P("tensor", "dp"),
            P("dp", None, "tensor"),
            P("tensor", "dp"),
            P("dp", "tensor", None),
        ),
        out_specs=(
            P("dp", "tensor", None),
            P("dp", "tensor", None),
            P("dp"),
            P("dp"),
            P("dp", None, "tensor"),
            P("tensor", "dp"),
            P("dp", None, "tensor"),
            P("tensor", "dp"),
        ),
        check_vma=False,
    )
```

```python
import functools
import math

import jax
import jax.numpy as jnp
from jax import lax
from jax.experimental import pallas as pl
from jax.experimental.pallas import tpu as pltpu
from jax.sharding import PartitionSpec as P

HD = 64
WINDOW = 128
REACH = WINDOW // 2
EPSILON = 1e-05
MASKED = -1e30
ROOT_HALF = 0.7071067811865476
DENSITY = 0.3989422804014327
BOTH = ("dp", "tensor")
GAIN_ROWS = 16
CHUNKS = 2
NN = (((1,), (0,)), ((), ()))
NT = (((1,), (1,)), ((), ()))
TN = (((0,), (0,)), ((), ()))


def mm(left, right, dims):
    return lax.dot_general(left, right, dims, preferred_element_type=jnp.float32)


def norm_rows(values):
    centre = values - jnp.mean(values, axis=-1, keepdims=True)
    variance = jnp.mean(centre * centre, axis=-1, keepdims=True)
    inverse = lax.rsqrt(variance + EPSILON)
    return centre * inverse, inverse


def norm_back(upstream, normed, inverse, gain):
    scaled = upstream * gain
    inner = (
        scaled
        - jnp.mean(scaled, axis=-1, keepdims=True)
        - normed * jnp.mean(scaled * normed, axis=-1, keepdims=True)
    )
    return inverse * inner


def plans(dps, tensors):
    dp_bits = [("dp", j) for j in range(dps.bit_length() - 1)]
    t_bits = [("tensor", j) for j in range(tensors.bit_length() - 1)]
    core, ys = dp_bits[:1], dp_bits[1:]
    xs, z_near, z_far = t_bits[:1], t_bits[1:2], t_bits[2:]
    return (
        core + ys + xs + z_near + z_far,
        core + xs + z_near + ys + z_far,
        core + z_near + ys + xs + z_far,
        core + ys + xs + z_near + z_far,
    )


def at_block(order, d):
    return tuple((d >> j) & 1 if axis == "dp" else 0 for axis, j in order)


def wide(order, dps, ref, part):
    return jnp.concatenate([ref[at_block(order, d) + (part,)] for d in range(dps)], axis=1)


def spread(order, dps, ref, part, value):
    rows = ref.shape[-1]
    for d in range(dps):
        ref[at_block(order, d) + (part,)] = value[:, d * rows : (d + 1) * rows].astype(ref.dtype)


def bit_of(axis, j):
    return (lax.axis_index(axis) // 2**j) % 2


def partner(axis, j):
    moved = {name: lax.axis_index(name) for name in BOTH}
    moved[axis] = moved[axis] + 2**j * (1 - 2 * bit_of(axis, j))
    return tuple(moved[name] for name in BOTH)


def greet(order):
    barrier = pltpu.get_barrier_semaphore()
    for axis, j in order:
        pl.semaphore_signal(
            barrier, inc=1, device_id=partner(axis, j), device_id_type=pl.DeviceIdType.MESH
        )
    pl.semaphore_wait(barrier, len(order))


def gather_kernel(orders, *refs):
    count = len(orders)
    ins, outs = refs[:count], refs[count : 2 * count]
    load_sem, send_sem, recv_sem = refs[2 * count :]
    bits = len(orders[0])
    greet(orders[0])
    spots = []
    for i, order in enumerate(orders):
        spot = 0
        for s, (axis, j) in enumerate(order):
            spot = spot + bit_of(axis, j) * 2 ** (bits - 1 - s)
        spots.append(spot)
    loads = [
        pltpu.make_async_copy(ins[i], outs[i].at[pl.ds(spots[i], 1)], load_sem.at[i])
        for i in range(count)
    ]
    for load in loads:
        load.start()
    for s in range(bits - 1, -1, -1):
        size = 2 ** (bits - 1 - s)
        copies = []
        for i, order in enumerate(orders):
            base = (spots[i] // size) * size
            span = outs[i].at[pl.ds(base, size)]
            copy = pltpu.make_async_remote_copy(
                src_ref=ins[i] if size == 1 else span,
                dst_ref=span,
                send_sem=send_sem.at[i, s],
                recv_sem=recv_sem.at[i, s],
                device_id=partner(*order[s]),
                device_id_type=pl.DeviceIdType.MESH,
            )
            copy.start()
            copies.append(copy)
        if s == bits - 1:
            for load in loads:
                load.wait()
        for copy in copies:
            copy.wait()


def gather_all(orders, dps, tensors, shards):
    bits = len(orders[0])
    group = dps * tensors
    count = len(shards)
    return pl.pallas_call(
        functools.partial(gather_kernel, orders),
        in_specs=[pl.BlockSpec(memory_space=pltpu.VMEM)] * count,
        out_specs=[pl.BlockSpec(memory_space=pl.ANY)] * count,
        out_shape=[jax.ShapeDtypeStruct((group,) + x.shape, x.dtype) for x in shards],
        scratch_shapes=[
            pltpu.SemaphoreType.DMA((count,)),
            pltpu.SemaphoreType.DMA((count, bits)),
            pltpu.SemaphoreType.DMA((count, bits)),
        ],
        compiler_params=pltpu.CompilerParams(collective_id=0, has_side_effects=True),
        name="gather_all",
    )(*[x[None] for x in shards])


def scatter_kernel(orders, *refs):
    count = len(orders)
    bits = len(orders[0])
    ins, outs = refs[:count], refs[count : 2 * count]
    lands, owns = refs[2 * count : 3 * count], refs[3 * count : 4 * count]
    load_sem, send_sem, recv_sem = refs[4 * count :]
    greet(orders[0])
    sizes = [2 ** (bits - 1 - s) for s in range(bits)]
    offsets = [sum(sizes[:s]) for s in range(bits)]

    def send(i, s, base):
        axis, j = orders[i][s]
        other = base + (1 - bit_of(axis, j)) * sizes[s]
        source = ins[i] if s == 0 else lands[i]
        copy = pltpu.make_async_remote_copy(
            src_ref=source.at[pl.ds(other, sizes[s])],
            dst_ref=lands[i].at[pl.ds(offsets[s], sizes[s])],
            send_sem=send_sem.at[i, s],
            recv_sem=recv_sem.at[i, s],
            device_id=partner(axis, j),
            device_id_type=pl.DeviceIdType.MESH,
        )
        copy.start()
        return copy

    def add(i, s, base, first, size):
        def one(k, carry):
            mine = lands[i][base + first + k].astype(jnp.float32)
            theirs = lands[i][offsets[s] + first + k].astype(jnp.float32)
            lands[i][base + first + k] = (mine + theirs).astype(lands[i].dtype)
            return carry

        lax.fori_loop(0, size, one, 0)

    copies = [send(i, 0, 0) for i in range(count)]
    piece = owns[0].shape[1]
    pieces = sizes[0] // piece

    def start_of(i, c):
        return ((1 - bit_of(*orders[i][1])) * sizes[1] + c * piece) % sizes[0]

    def load(i, c):
        kept = bit_of(*orders[i][0]) * sizes[0] + start_of(i, c)
        copy = pltpu.make_async_copy(
            ins[i].at[pl.ds(kept, piece)], owns[i].at[c % 2], load_sem.at[i, c % 2]
        )
        copy.start()
        return copy

    loads = [[load(i, c) for c in range(2)] for i in range(count)]
    for copy in copies:
        copy.wait()
    later = []
    for c in range(pieces):
        for i in range(count):
            loads[i][c].wait()
            at = start_of(i, c)

            def one(k, carry, i=i, c=c, at=at):
                mine = owns[i][c % 2, k].astype(jnp.float32)
                theirs = lands[i][at + k].astype(jnp.float32)
                lands[i][at + k] = (mine + theirs).astype(lands[i].dtype)
                return carry

            lax.fori_loop(0, piece, one, 0)
            if c + 2 < pieces:
                loads[i].append(load(i, c + 2))
            if c == pieces // 2 - 1:
                later.append(send(i, 1, 0))
    bases = [bit_of(*orders[i][1]) * sizes[1] for i in range(count)]
    copies = later
    for s in range(1, bits):
        later = []
        for i in range(count):
            copies[i].wait()
            if s == bits - 1:
                mine = lands[i][bases[i]].astype(jnp.float32)
                theirs = lands[i][offsets[s]].astype(jnp.float32)
                outs[i][...] = mine + theirs
                continue
            bit = bit_of(*orders[i][s + 1])
            half = sizes[s + 1]
            add(i, s, bases[i], (1 - bit) * half, half)
            later.append(send(i, s + 1, bases[i]))
        for i in range(count):
            if s < bits - 1:
                bit = bit_of(*orders[i][s + 1])
                half = sizes[s + 1]
                add(i, s, bases[i], bit * half, half)
                bases[i] = bases[i] + bit * half
        copies = later


def scatter_all(orders, dps, tensors, parts):
    bits = len(orders[0])
    group = dps * tensors
    count = len(parts)
    return pl.pallas_call(
        functools.partial(scatter_kernel, orders),
        in_specs=[pl.BlockSpec(memory_space=pl.ANY)] * count,
        out_specs=[pl.BlockSpec(memory_space=pltpu.VMEM)] * count,
        out_shape=[jax.ShapeDtypeStruct(x.shape[1:], jnp.float32) for x in parts],
        scratch_shapes=[pltpu.VMEM((group - 1,) + x.shape[1:], x.dtype) for x in parts]
        + [pltpu.VMEM((2, max(group // 16, 1)) + x.shape[1:], x.dtype) for x in parts]
        + [
            pltpu.SemaphoreType.DMA((count, 2)),
            pltpu.SemaphoreType.DMA((count, bits)),
            pltpu.SemaphoreType.DMA((count, bits)),
        ],
        compiler_params=pltpu.CompilerParams(
            collective_id=1, has_side_effects=True, vmem_limit_bytes=60 * 1024 * 1024
        ),
        name="scatter_all",
    )(*parts)


def turn(tensor, first_sign):
    half = HD // 2
    pieces = []
    for head in range(tensor.shape[1] // HD):
        low = tensor[:, head * HD : head * HD + half]
        high = tensor[:, head * HD + half : (head + 1) * HD]
        pieces += [-high, low] if first_sign < 0 else [high, -low]
    return jnp.concatenate(pieces, axis=1)


def blocks_of(tokens):
    size = min(tokens, 128)
    return [(start, size, size + 2 * REACH) for start in range(0, tokens, size)]


def band_mask(segq, segk, start, size, span):
    rows = lax.broadcasted_iota(jnp.int32, (size, span), 0)
    cols = lax.broadcasted_iota(jnp.int32, (size, span), 1)
    near = jnp.abs(rows + REACH - cols) <= REACH
    return near & (segq[start : start + size, :] == segk[:, start : start + span])


def attend_kernel(order, dps, x_ref, gain_ref, w_ref, cos_ref, sin_ref, segq_ref, segk_ref,
                  y_ref, qkv_ref, ctx_ref, lse_ref, a_ref):
    step = pl.program_id(0)
    tokens = y_ref.shape[0]
    scale = HD ** (-0.5)

    @pl.when(step == 0)
    def _():
        normed, _ = norm_rows(x_ref[...])
        a_ref[...] = (normed * gain_ref[...].astype(jnp.float32)).astype(jnp.bfloat16)
        y_ref[...] = x_ref[REACH : REACH + tokens, :]

    a = a_ref[...]
    cos, sin = cos_ref[...], sin_ref[...]
    q = mm(a, wide(order, dps, w_ref, 0), NT)
    k = mm(a, wide(order, dps, w_ref, 1), NT)
    v = mm(a, wide(order, dps, w_ref, 2), NT).astype(jnp.bfloat16)
    q = (q * cos + turn(q, -1) * sin).astype(jnp.bfloat16)
    k = (k * cos + turn(k, -1) * sin).astype(jnp.bfloat16)
    qkv_ref[0, 0], qkv_ref[0, 1], qkv_ref[0, 2] = q, k, v
    heads = q.shape[1] // HD
    segq, segk = segq_ref[...], segk_ref[...]
    contexts, totals = [], []
    for start, size, span in blocks_of(tokens):
        valid = band_mask(segq, segk, start, size, span)
        row_ctx, row_lse = [], []
        for head in range(heads):
            lanes = slice(head * HD, (head + 1) * HD)
            qb = q[REACH + start : REACH + start + size, lanes]
            kb = k[start : start + span, lanes]
            vb = v[start : start + span, lanes]
            s = jnp.where(valid, mm(qb, kb, NT) * scale, MASKED)
            peak = jnp.max(s, axis=-1, keepdims=True)
            total = peak + jnp.log(jnp.sum(jnp.exp(s - peak), axis=-1, keepdims=True))
            weights = jnp.exp(s - total).astype(jnp.bfloat16)
            row_ctx.append(mm(weights, vb, NN))
            row_lse.append(total)
        contexts.append(jnp.concatenate(row_ctx, axis=1))
        totals.append(jnp.concatenate(row_lse, axis=1))
    context = jnp.concatenate(contexts, axis=0).astype(jnp.bfloat16)
    ctx_ref[0] = context
    lse_ref[0] = jnp.concatenate(totals, axis=0)
    y_ref[...] += mm(context, wide(order, dps, w_ref, 3), NN)


def attend_back_kernel(order, dps, x_ref, gain_ref, w_ref, cos_ref, sin_ref, segq_ref, segk_ref,
                       qkv_ref, ctx_ref, lse_ref, dy_ref,
                       dw_ref, da_ref, gg_ref, a_ref, n_ref, d_ref):
    step = pl.program_id(0)
    tokens = dy_ref.shape[0]
    scale = HD ** (-0.5)

    @pl.when(step == 0)
    def _():
        normed, _ = norm_rows(x_ref[...])
        n_ref[...] = normed
        a_ref[...] = (normed * gain_ref[...].astype(jnp.float32)).astype(jnp.bfloat16)
        d_ref[...] = dy_ref[...].astype(jnp.bfloat16)
        da_ref[...] = jnp.zeros_like(da_ref)

    dyb = d_ref[...]
    dc = mm(dyb, wide(order, dps, w_ref, 3), NT).astype(jnp.bfloat16)
    spread(order, dps, dw_ref, 3, mm(ctx_ref[0], dyb, TN))
    q, k, v = qkv_ref[0, 0], qkv_ref[0, 1], qkv_ref[0, 2]
    heads = q.shape[1] // HD
    segq, segk = segq_ref[...], segk_ref[...]
    lse = lse_ref[0]
    extent = tokens + 2 * REACH
    width = q.shape[1]
    dq_rows = []
    dk = jnp.zeros((extent, width), jnp.float32)
    dv = jnp.zeros((extent, width), jnp.float32)
    for start, size, span in blocks_of(tokens):
        valid = band_mask(segq, segk, start, size, span)
        dq_parts, dk_parts, dv_parts = [], [], []
        for head in range(heads):
            lanes = slice(head * HD, (head + 1) * HD)
            qb = q[REACH + start : REACH + start + size, lanes]
            kb = k[start : start + span, lanes]
            vb = v[start : start + span, lanes]
            db = dc[start : start + size, lanes]
            s = jnp.where(valid, mm(qb, kb, NT) * scale, MASKED)
            probs = jnp.exp(s - lse[start : start + size, head : head + 1])
            dp = mm(db, vb, NT)
            delta = jnp.sum(probs * dp, axis=-1, keepdims=True)
            ds = (probs * (dp - delta) * scale).astype(jnp.bfloat16)
            dq_parts.append(mm(ds, kb, NN))
            dk_parts.append(mm(ds, qb, TN))
            dv_parts.append(mm(probs.astype(jnp.bfloat16), db, TN))
        dq_rows.append(jnp.concatenate(dq_parts, axis=1))
        pads = ((start, extent - start - span), (0, 0))
        for parts, which in ((dk_parts, 0), (dv_parts, 1)):
            block = jnp.concatenate(parts, axis=1)
            rows = []
            if pads[0][0]:
                rows.append(jnp.zeros((pads[0][0], width), jnp.float32))
            rows.append(block)
            if pads[0][1]:
                rows.append(jnp.zeros((pads[0][1], width), jnp.float32))
            block = jnp.concatenate(rows, axis=0) if len(rows) > 1 else block
            if which == 0:
                dk = dk + block
            else:
                dv = dv + block
    cos, sin = cos_ref[...], sin_ref[...]
    dq = jnp.concatenate(dq_rows, axis=0)
    inner = slice(REACH, REACH + tokens)
    dq = (dq * cos[inner] + turn(dq * sin[inner], 1)).astype(jnp.bfloat16)
    dk = (dk * cos + turn(dk * sin, 1)).astype(jnp.bfloat16)
    dv = dv.astype(jnp.bfloat16)
    a = a_ref[...]
    spread(order, dps, dw_ref, 0, mm(dq, a[inner], TN))
    spread(order, dps, dw_ref, 1, mm(dk, a, TN))
    spread(order, dps, dw_ref, 2, mm(dv, a, TN))
    da_ref[...] += mm(dk, wide(order, dps, w_ref, 1), NN) + mm(dv, wide(order, dps, w_ref, 2), NN)
    da_ref[inner, :] += mm(dq, wide(order, dps, w_ref, 0), NN)

    @pl.when(step == pl.num_programs(0) - 1)
    def _():
        gg_ref[...] = jnp.sum(da_ref[...] * n_ref[...], axis=0, keepdims=True)


def feed_kernel(order, dps, y_ref, gain_ref, up_ref, w_ref, out0_ref, da0_ref,
                dw_ref, out_ref, da_ref, a_ref, u_ref):
    step = pl.program_id(0)

    @pl.when(step == 0)
    def _():
        normed, _ = norm_rows(y_ref[...])
        a_ref[...] = (normed * gain_ref[...].astype(jnp.float32)).astype(jnp.bfloat16)
        u_ref[...] = up_ref[...].astype(jnp.bfloat16)
        out_ref[...] = out0_ref[...]
        da_ref[...] = da0_ref[...]

    a, up = a_ref[...], u_ref[...]
    w0, w1, c = wide(order, dps, w_ref, 0), wide(order, dps, w_ref, 1), wide(order, dps, w_ref, 2)
    u0 = mm(w0, a, NT)
    u1 = mm(w1, a, NT)
    cdf = 0.5 * (1.0 + lax.erf(u0 * ROOT_HALF))
    activated = u0 * cdf
    slope = cdf + u0 * DENSITY * jnp.exp(-0.5 * u0 * u0)
    hidden = (activated * u1).astype(jnp.bfloat16)
    out_ref[...] += mm(hidden, c, TN)
    spread(order, dps, dw_ref, 2, mm(hidden, up, NN))
    dg = mm(c, up, NT)
    du0 = (dg * u1 * slope).astype(jnp.bfloat16)
    du1 = (dg * activated).astype(jnp.bfloat16)
    spread(order, dps, dw_ref, 0, mm(du0, a, NN))
    spread(order, dps, dw_ref, 1, mm(du1, a, NN))
    da_ref[...] += mm(du0, w0, TN) + mm(du1, w1, TN)


def full_spec(shape):
    return pl.BlockSpec(shape, lambda t: (0,) * len(shape))


def weight_spec(order, block):
    lead = tuple(2 if axis == "dp" else 1 for axis, _ in order)

    def place(t):
        return tuple(0 if axis == "dp" else (t // 2**j) % 2 for axis, j in order) + (0,) * len(block)

    return pl.BlockSpec(lead + block, place)


def lead_spec(shape):
    return pl.BlockSpec((1,) + shape[1:], lambda t: (t,) + (0,) * (len(shape) - 1))


def params():
    return pltpu.CompilerParams(
        dimension_semantics=("arbitrary",), vmem_limit_bytes=56 * 1024 * 1024
    )


def shaped(shape, dtype):
    return jax.ShapeDtypeStruct(shape, dtype)


def cost(flops, moved):
    return pl.CostEstimate(flops=int(flops), bytes_accessed=int(moved), transcendentals=0)


def body(
    dps,
    tensors,
    block_input,
    segment_ids,
    positions,
    attention_gain,
    feedforward_gain,
    qkv_weight,
    output_weight,
    expand_weight,
    contract_weight,
    cotangent,
):
    tokens, width = block_input.shape[1:]
    rows = qkv_weight.shape[0]
    hw = qkv_weight.shape[2]
    units = contract_weight.shape[0]
    heads = hw // HD
    extent = tokens + 2 * REACH
    f32, bf16 = jnp.float32, jnp.bfloat16

    x = block_input[0]
    upstream = cotangent[0]
    place = lax.axis_index("tensor")
    ahead = [(i, i + 1) for i in range(tensors - 1)]
    behind = [(i + 1, i) for i in range(tensors - 1)]
    before = lax.ppermute(x[tokens - REACH :], "tensor", ahead)
    after = lax.ppermute(x[:REACH], "tensor", behind)
    x_ext = jnp.concatenate([before, x, after], axis=0)

    orders = plans(dps, tensors)
    group = dps * tensors
    bits = len(orders[0])
    split = (2,) * bits
    gains = jnp.pad(jnp.stack([attention_gain, feedforward_gain]), ((0, GAIN_ROWS - 2), (0, 0)))
    first = jnp.concatenate(
        [jnp.transpose(qkv_weight, (1, 2, 0)), output_weight[None]], axis=0
    )
    stacked = jnp.concatenate(
        [jnp.transpose(expand_weight, (1, 2, 0)), contract_weight[None]], axis=0
    )
    cut = -(-units // (8 * CHUNKS)) * 8
    edges = [min(i * cut, units) for i in range(CHUNKS + 1)]
    shards = [first] + [stacked[:, lo:hi] for lo, hi in zip(edges[:-1], edges[1:])] + [gains]
    got_first, *got_feed, got_gains = gather_all(orders, dps, tensors, shards)
    w_attn = got_first.reshape(split + first.shape)
    at_zero = jnp.stack(
        [got_gains.reshape(split + gains.shape)[at_block(orders[3], d)] for d in range(dps)]
    )
    gain_one = at_zero[:, 0].reshape(1, width)
    gain_two = at_zero[:, 1].reshape(1, width)

    seg_all = jnp.pad(segment_ids[0], (REACH, REACH), constant_values=-1)
    pos_all = jnp.pad(positions[0], (REACH, REACH))
    seg_k = lax.dynamic_slice_in_dim(seg_all, place * tokens, extent, 0)
    pos = lax.dynamic_slice_in_dim(pos_all, place * tokens, extent, 0)
    seg_q = seg_k[REACH : REACH + tokens]
    half = HD // 2
    frequency = jnp.exp(jnp.arange(half, dtype=f32) * (-2.0 * math.log(10000.0) / HD))
    angles = pos.astype(f32)[:, None] * frequency[None, :]
    cos = jnp.tile(jnp.cos(angles), (1, 2 * heads))
    sin = jnp.tile(jnp.sin(angles), (1, 2 * heads))
    seg_q, seg_k = seg_q[:, None], seg_k[None, :]

    w_block = first.shape
    side = [
        full_spec((extent, width)),
        full_spec((1, width)),
        weight_spec(orders[0], w_block),
        full_spec((extent, hw)),
        full_spec((extent, hw)),
        full_spec((tokens, 1)),
        full_spec((1, extent)),
    ]
    qkv_shape = (tensors, 3, extent, hw)
    ctx_shape = (tensors, tokens, hw)
    lse_shape = (tensors, tokens, heads)
    attn_flops = 2 * tensors * extent * 4 * hw * width
    attn_bytes = 2 * 4 * width * width
    y, qkv, ctx, lse = pl.pallas_call(
        functools.partial(attend_kernel, orders[0], dps),
        grid=(tensors,),
        in_specs=side,
        out_specs=[
            full_spec((tokens, width)),
            lead_spec(qkv_shape),
            lead_spec(ctx_shape),
            lead_spec(lse_shape),
        ],
        out_shape=[
            shaped((tokens, width), f32),
            shaped(qkv_shape, bf16),
            shaped(ctx_shape, bf16),
            shaped(lse_shape, f32),
        ],
        scratch_shapes=[pltpu.VMEM((extent, width), bf16)],
        compiler_params=params(),
        cost_estimate=cost(attn_flops, attn_bytes),
        name="attend",
    )(x_ext, gain_one, w_attn, cos, sin, seg_q, seg_k)

    out, da_two = y, jnp.zeros((tokens, width), f32)
    feed_grads = []
    for order, got in zip(orders[1:], got_feed):
        block = got.shape[1:]
        size = block[1]
        got = got.reshape(split + block)
        dw, out, da_two = pl.pallas_call(
            functools.partial(feed_kernel, order, dps),
            grid=(tensors,),
            in_specs=[
                full_spec((tokens, width)),
                full_spec((1, width)),
                full_spec((tokens, width)),
                weight_spec(order, block),
                full_spec((tokens, width)),
                full_spec((tokens, width)),
            ],
            out_specs=[
                weight_spec(order, block),
                full_spec((tokens, width)),
                full_spec((tokens, width)),
            ],
            out_shape=[
                shaped(got.shape, bf16),
                shaped((tokens, width), f32),
                shaped((tokens, width), f32),
            ],
            scratch_shapes=[
                pltpu.VMEM((tokens, width), bf16),
                pltpu.VMEM((tokens, width), bf16),
            ],
            compiler_params=params(),
            cost_estimate=cost(18 * tensors * tokens * size * width, 12 * tensors * size * width),
            name="feed",
        )(y, gain_two, upstream, got, out, da_two)
        feed_grads.append(dw.reshape((group,) + block))

    normed_two, inverse_two = norm_rows(y)
    gain_grad_two = jnp.sum(da_two * normed_two, axis=0)
    grad_mid = upstream + norm_back(da_two, normed_two, inverse_two, gain_two.astype(f32))

    dw_attn, da_one, gain_grad_one = pl.pallas_call(
        functools.partial(attend_back_kernel, orders[0], dps),
        grid=(tensors,),
        in_specs=side
        + [
            lead_spec(qkv_shape),
            lead_spec(ctx_shape),
            lead_spec(lse_shape),
            full_spec((tokens, width)),
        ],
        out_specs=[
            weight_spec(orders[0], w_block),
            full_spec((extent, width)),
            full_spec((1, width)),
        ],
        out_shape=[
            shaped(split + w_block, bf16),
            shaped((extent, width), f32),
            shaped((1, width), f32),
        ],
        scratch_shapes=[
            pltpu.VMEM((extent, width), bf16),
            pltpu.VMEM((extent, width), f32),
            pltpu.VMEM((tokens, width), bf16),
        ],
        compiler_params=params(),
        cost_estimate=cost(2 * attn_flops, 2 * attn_bytes),
        name="attend_back",
    )(x_ext, gain_one, w_attn, cos, sin, seg_q, seg_k, qkv, ctx, lse, grad_mid)

    gain_grads = jnp.stack([gain_grad_one[0], gain_grad_two]).reshape(2, dps, rows)
    gain_block = jnp.pad(jnp.transpose(gain_grads, (1, 0, 2)), ((0, 0), (0, 6), (0, 0)))
    gain_block = gain_block.reshape(
        tuple(2 for _ in range(dps.bit_length() - 1)) + (1,) * (tensors.bit_length() - 1) + (8, rows)
    )
    names = [("dp", j) for j in range(dps.bit_length() - 2, -1, -1)]
    names += [("tensor", j) for j in range(tensors.bit_length() - 2, -1, -1)]
    spots = [names.index(bit) for bit in orders[3]]
    gain_block = jnp.broadcast_to(
        jnp.transpose(gain_block, spots + [bits, bits + 1]), split + (8, rows)
    ).reshape(group, 8, rows)
    owned, *owned_feed, owned_gains = scatter_all(
        orders, dps, tensors, [dw_attn.reshape((group,) + w_block)] + feed_grads + [gain_block]
    )

    to_before = lax.ppermute(da_one[:REACH].astype(bf16), "tensor", behind).astype(f32)
    to_after = lax.ppermute(da_one[tokens + REACH :].astype(bf16), "tensor", ahead).astype(f32)
    da_total = da_one[REACH : REACH + tokens]
    da_total = da_total + jnp.concatenate(
        [to_after, jnp.zeros((tokens - 2 * REACH, width), f32), to_before], axis=0
    )
    normed_one, inverse_one = norm_rows(x)
    input_grad = grad_mid + norm_back(da_total, normed_one, inverse_one, gain_one.astype(f32))

    feed = jnp.concatenate(owned_feed, axis=1)
    return (
        out[None],
        input_grad[None],
        owned_gains[0],
        owned_gains[1],
        jnp.transpose(owned[:3], (2, 0, 1)),
        owned[3],
        jnp.transpose(feed[:2], (2, 0, 1)),
        feed[2],
    )


def solution(mesh):
    return jax.shard_map(
        functools.partial(body, mesh.shape["dp"], mesh.shape["tensor"]),
        mesh=mesh,
        in_specs=(
            P("dp", "tensor", None),
            P("dp", None),
            P("dp", None),
            P("dp"),
            P("dp"),
            P("dp", None, "tensor"),
            P("tensor", "dp"),
            P("dp", None, "tensor"),
            P("tensor", "dp"),
            P("dp", "tensor", None),
        ),
        out_specs=(
            P("dp", "tensor", None),
            P("dp", "tensor", None),
            P("dp"),
            P("dp"),
            P("dp", None, "tensor"),
            P("tensor", "dp"),
            P("dp", None, "tensor"),
            P("tensor", "dp"),
        ),
        check_vma=False,
    )
```

```python
import functools
import math

import jax
import jax.numpy as jnp
from jax import lax
from jax.experimental import pallas as pl
from jax.experimental.pallas import tpu as pltpu
from jax.sharding import PartitionSpec as P

HD = 64
WINDOW = 128
REACH = WINDOW // 2
EPSILON = 1e-05
MASKED = -1e30
ROOT_HALF = 0.7071067811865476
DENSITY = 0.3989422804014327
BOTH = ("dp", "tensor")
GAIN_ROWS = 16
CHUNKS = 2
NN = (((1,), (0,)), ((), ()))
NT = (((1,), (1,)), ((), ()))
TN = (((0,), (0,)), ((), ()))


def mm(left, right, dims):
    return lax.dot_general(left, right, dims, preferred_element_type=jnp.float32)


def norm_rows(values):
    centre = values - jnp.mean(values, axis=-1, keepdims=True)
    variance = jnp.mean(centre * centre, axis=-1, keepdims=True)
    inverse = lax.rsqrt(variance + EPSILON)
    return centre * inverse, inverse


def norm_back(upstream, normed, inverse, gain):
    scaled = upstream * gain
    inner = (
        scaled
        - jnp.mean(scaled, axis=-1, keepdims=True)
        - normed * jnp.mean(scaled * normed, axis=-1, keepdims=True)
    )
    return inverse * inner


def plans(dps, tensors):
    dp_bits = [("dp", j) for j in range(dps.bit_length() - 1)]
    t_bits = [("tensor", j) for j in range(tensors.bit_length() - 1)]
    core, ys = dp_bits[:1], dp_bits[1:]
    xs, z_near, z_far = t_bits[:1], t_bits[1:2], t_bits[2:]
    return (
        core + ys + xs + z_near + z_far,
        core + xs + z_near + ys + z_far,
        core + z_near + ys + xs + z_far,
        core + ys + xs + z_near + z_far,
    )


def at_block(order, d):
    return tuple((d >> j) & 1 if axis == "dp" else 0 for axis, j in order)


def wide(order, dps, ref, part):
    return jnp.concatenate([ref[at_block(order, d) + (part,)] for d in range(dps)], axis=1)


def spread(order, dps, ref, part, value):
    rows = ref.shape[-1]
    for d in range(dps):
        ref[at_block(order, d) + (part,)] = value[:, d * rows : (d + 1) * rows].astype(ref.dtype)


def bit_of(axis, j):
    return (lax.axis_index(axis) // 2**j) % 2


def partner(axis, j):
    moved = {name: lax.axis_index(name) for name in BOTH}
    moved[axis] = moved[axis] + 2**j * (1 - 2 * bit_of(axis, j))
    return tuple(moved[name] for name in BOTH)


def greet(order):
    barrier = pltpu.get_barrier_semaphore()
    for axis, j in order:
        pl.semaphore_signal(
            barrier, inc=1, device_id=partner(axis, j), device_id_type=pl.DeviceIdType.MESH
        )
    pl.semaphore_wait(barrier, len(order))


def gather_kernel(orders, *refs):
    count = len(orders)
    ins, outs = refs[:count], refs[count : 2 * count]
    load_sem, send_sem, recv_sem = refs[2 * count :]
    bits = len(orders[0])
    greet(orders[0])
    spots = []
    for i, order in enumerate(orders):
        spot = 0
        for s, (axis, j) in enumerate(order):
            spot = spot + bit_of(axis, j) * 2 ** (bits - 1 - s)
        spots.append(spot)
    loads = [
        pltpu.make_async_copy(ins[i], outs[i].at[pl.ds(spots[i], 1)], load_sem.at[i])
        for i in range(count)
    ]
    for load in loads:
        load.start()
    lanes = []
    for i in range(count):
        parts = outs[i].shape[1]
        cut = (parts + i % 2) // 2 if len(outs[i].shape) == 4 else parts
        lanes.append((0, i, pl.ds(0, cut)))
        if cut < parts:
            lanes.append((1, i, pl.ds(cut, parts - cut)))
    lanes.sort(key=lambda lane: lane[:2])
    flying = {}
    for s in range(bits - 1, -1, -1):
        size = 2 ** (bits - 1 - s)
        for group, i, rows in lanes:
            if (group, i) in flying:
                flying[group, i].wait()
            span = outs[i].at[pl.ds((spots[i] // size) * size, size), rows]
            copy = pltpu.make_async_remote_copy(
                src_ref=ins[i].at[pl.ds(0, 1), rows] if size == 1 else span,
                dst_ref=span,
                send_sem=send_sem.at[group, i, s],
                recv_sem=recv_sem.at[group, i, s],
                device_id=partner(*orders[i][s]),
                device_id_type=pl.DeviceIdType.MESH,
            )
            copy.start()
            flying[group, i] = copy
        if s == bits - 1:
            for load in loads:
                load.wait()
    for copy in flying.values():
        copy.wait()


def gather_all(orders, dps, tensors, shards):
    bits = len(orders[0])
    group = dps * tensors
    count = len(shards)
    return pl.pallas_call(
        functools.partial(gather_kernel, orders),
        in_specs=[pl.BlockSpec(memory_space=pltpu.VMEM)] * count,
        out_specs=[pl.BlockSpec(memory_space=pl.ANY)] * count,
        out_shape=[jax.ShapeDtypeStruct((group,) + x.shape, x.dtype) for x in shards],
        scratch_shapes=[
            pltpu.SemaphoreType.DMA((count,)),
            pltpu.SemaphoreType.DMA((2, count, bits)),
            pltpu.SemaphoreType.DMA((2, count, bits)),
        ],
        compiler_params=pltpu.CompilerParams(collective_id=0, has_side_effects=True),
        cost_estimate=cost(0, 3 * 10**8),
        name="gather_all",
    )(*[x[None] for x in shards])


def scatter_kernel(orders, *refs):
    count = len(orders)
    bits = len(orders[0])
    ins, outs = refs[:count], refs[count : 2 * count]
    lands, owns = refs[2 * count : 3 * count], refs[3 * count : 4 * count]
    load_sem, send_sem, recv_sem = refs[4 * count :]
    greet(orders[0])
    sizes = [2 ** (bits - 1 - s) for s in range(bits)]
    offsets = [sum(sizes[:s]) for s in range(bits)]

    def send(i, s, base):
        axis, j = orders[i][s]
        other = base + (1 - bit_of(axis, j)) * sizes[s]
        source = ins[i] if s == 0 else lands[i]
        copy = pltpu.make_async_remote_copy(
            src_ref=source.at[pl.ds(other, sizes[s])],
            dst_ref=lands[i].at[pl.ds(offsets[s], sizes[s])],
            send_sem=send_sem.at[i, s],
            recv_sem=recv_sem.at[i, s],
            device_id=partner(axis, j),
            device_id_type=pl.DeviceIdType.MESH,
        )
        copy.start()
        return copy

    def add(i, s, base, first, size):
        def one(k, carry):
            mine = lands[i][base + first + k].astype(jnp.float32)
            theirs = lands[i][offsets[s] + first + k].astype(jnp.float32)
            lands[i][base + first + k] = (mine + theirs).astype(lands[i].dtype)
            return carry

        lax.fori_loop(0, size, one, 0)

    copies = [send(i, 0, 0) for i in range(count)]
    piece = owns[0].shape[1]
    pieces = sizes[0] // piece

    def start_of(i, c):
        return ((1 - bit_of(*orders[i][1])) * sizes[1] + c * piece) % sizes[0]

    def load(i, c):
        kept = bit_of(*orders[i][0]) * sizes[0] + start_of(i, c)
        copy = pltpu.make_async_copy(
            ins[i].at[pl.ds(kept, piece)], owns[i].at[c % 2], load_sem.at[i, c % 2]
        )
        copy.start()
        return copy

    loads = [[load(i, c) for c in range(2)] for i in range(count)]
    later = []
    for i in range(count):
        copies[i].wait()
        for c in range(pieces):
            loads[i][c].wait()
            at = start_of(i, c)

            def one(k, carry, i=i, c=c, at=at):
                mine = owns[i][c % 2, k].astype(jnp.float32)
                theirs = lands[i][at + k].astype(jnp.float32)
                lands[i][at + k] = (mine + theirs).astype(lands[i].dtype)
                return carry

            lax.fori_loop(0, piece, one, 0)
            if c + 2 < pieces:
                loads[i].append(load(i, c + 2))
            if c == pieces // 2 - 1:
                later.append(send(i, 1, 0))
    bases = [bit_of(*orders[i][1]) * sizes[1] for i in range(count)]
    copies = later
    for s in range(1, bits):
        later = []
        for i in range(count):
            copies[i].wait()
            if s == bits - 1:
                mine = lands[i][bases[i]].astype(jnp.float32)
                theirs = lands[i][offsets[s]].astype(jnp.float32)
                outs[i][...] = mine + theirs
                continue
            bit = bit_of(*orders[i][s + 1])
            half = sizes[s + 1]
            add(i, s, bases[i], (1 - bit) * half, half)
            later.append(send(i, s + 1, bases[i]))
        for i in range(count):
            if s < bits - 1:
                bit = bit_of(*orders[i][s + 1])
                half = sizes[s + 1]
                add(i, s, bases[i], bit * half, half)
                bases[i] = bases[i] + bit * half
        copies = later


def scatter_all(orders, dps, tensors, parts):
    bits = len(orders[0])
    group = dps * tensors
    count = len(parts)
    return pl.pallas_call(
        functools.partial(scatter_kernel, orders),
        in_specs=[pl.BlockSpec(memory_space=pl.ANY)] * count,
        out_specs=[pl.BlockSpec(memory_space=pltpu.VMEM)] * count,
        out_shape=[jax.ShapeDtypeStruct(x.shape[1:], jnp.float32) for x in parts],
        scratch_shapes=[pltpu.VMEM((group - 1,) + x.shape[1:], x.dtype) for x in parts]
        + [pltpu.VMEM((2, max(group // 16, 1)) + x.shape[1:], x.dtype) for x in parts]
        + [
            pltpu.SemaphoreType.DMA((count, 2)),
            pltpu.SemaphoreType.DMA((count, bits)),
            pltpu.SemaphoreType.DMA((count, bits)),
        ],
        compiler_params=pltpu.CompilerParams(
            collective_id=1, has_side_effects=True, vmem_limit_bytes=60 * 1024 * 1024
        ),
        cost_estimate=cost(0, 3 * 10**8),
        name="scatter_all",
    )(*parts)


def turn(tensor, first_sign):
    half = HD // 2
    pieces = []
    for head in range(tensor.shape[1] // HD):
        low = tensor[:, head * HD : head * HD + half]
        high = tensor[:, head * HD + half : (head + 1) * HD]
        pieces += [-high, low] if first_sign < 0 else [high, -low]
    return jnp.concatenate(pieces, axis=1)


def blocks_of(tokens):
    size = min(tokens, 128)
    return [(start, size, size + 2 * REACH) for start in range(0, tokens, size)]


def band_mask(segq, segk, start, size, span):
    rows = lax.broadcasted_iota(jnp.int32, (size, span), 0)
    cols = lax.broadcasted_iota(jnp.int32, (size, span), 1)
    near = jnp.abs(rows + REACH - cols) <= REACH
    return near & (segq[start : start + size, :] == segk[:, start : start + span])


def attend_kernel(order, dps, x_ref, gain_ref, w_ref, cos_ref, sin_ref, segq_ref, segk_ref,
                  y_ref, qkv_ref, ctx_ref, lse_ref, a_ref):
    step = pl.program_id(0)
    tokens = y_ref.shape[0]
    scale = HD ** (-0.5)

    @pl.when(step == 0)
    def _():
        normed, _ = norm_rows(x_ref[...])
        a_ref[...] = (normed * gain_ref[...].astype(jnp.float32)).astype(jnp.bfloat16)
        y_ref[...] = x_ref[REACH : REACH + tokens, :]

    a = a_ref[...]
    cos, sin = cos_ref[...], sin_ref[...]
    q = mm(a, wide(order, dps, w_ref, 0), NT)
    k = mm(a, wide(order, dps, w_ref, 1), NT)
    v = mm(a, wide(order, dps, w_ref, 2), NT).astype(jnp.bfloat16)
    q = (q * cos + turn(q, -1) * sin).astype(jnp.bfloat16)
    k = (k * cos + turn(k, -1) * sin).astype(jnp.bfloat16)
    qkv_ref[0, 0], qkv_ref[0, 1], qkv_ref[0, 2] = q, k, v
    heads = q.shape[1] // HD
    segq, segk = segq_ref[...], segk_ref[...]
    contexts, totals = [], []
    for start, size, span in blocks_of(tokens):
        valid = band_mask(segq, segk, start, size, span)
        row_ctx, row_lse = [], []
        for head in range(heads):
            lanes = slice(head * HD, (head + 1) * HD)
            qb = q[REACH + start : REACH + start + size, lanes]
            kb = k[start : start + span, lanes]
            vb = v[start : start + span, lanes]
            s = jnp.where(valid, mm(qb, kb, NT) * scale, MASKED)
            peak = jnp.max(s, axis=-1, keepdims=True)
            total = peak + jnp.log(jnp.sum(jnp.exp(s - peak), axis=-1, keepdims=True))
            weights = jnp.exp(s - total).astype(jnp.bfloat16)
            row_ctx.append(mm(weights, vb, NN))
            row_lse.append(total)
        contexts.append(jnp.concatenate(row_ctx, axis=1))
        totals.append(jnp.concatenate(row_lse, axis=1))
    context = jnp.concatenate(contexts, axis=0).astype(jnp.bfloat16)
    ctx_ref[0] = context
    lse_ref[0] = jnp.concatenate(totals, axis=0)
    y_ref[...] += mm(context, wide(order, dps, w_ref, 3), NN)


def attend_back_kernel(order, dps, x_ref, gain_ref, w_ref, cos_ref, sin_ref, segq_ref, segk_ref,
                       qkv_ref, ctx_ref, lse_ref, dy_ref,
                       dw_ref, da_ref, gg_ref, a_ref, n_ref, d_ref):
    step = pl.program_id(0)
    tokens = dy_ref.shape[0]
    scale = HD ** (-0.5)

    @pl.when(step == 0)
    def _():
        normed, _ = norm_rows(x_ref[...])
        n_ref[...] = normed
        a_ref[...] = (normed * gain_ref[...].astype(jnp.float32)).astype(jnp.bfloat16)
        d_ref[...] = dy_ref[...].astype(jnp.bfloat16)
        da_ref[...] = jnp.zeros_like(da_ref)

    dyb = d_ref[...]
    dc = mm(dyb, wide(order, dps, w_ref, 3), NT).astype(jnp.bfloat16)
    spread(order, dps, dw_ref, 3, mm(ctx_ref[0], dyb, TN))
    q, k, v = qkv_ref[0, 0], qkv_ref[0, 1], qkv_ref[0, 2]
    heads = q.shape[1] // HD
    segq, segk = segq_ref[...], segk_ref[...]
    lse = lse_ref[0]
    extent = tokens + 2 * REACH
    width = q.shape[1]
    dq_rows = []
    dk = jnp.zeros((extent, width), jnp.float32)
    dv = jnp.zeros((extent, width), jnp.float32)
    for start, size, span in blocks_of(tokens):
        valid = band_mask(segq, segk, start, size, span)
        dq_parts, dk_parts, dv_parts = [], [], []
        for head in range(heads):
            lanes = slice(head * HD, (head + 1) * HD)
            qb = q[REACH + start : REACH + start + size, lanes]
            kb = k[start : start + span, lanes]
            vb = v[start : start + span, lanes]
            db = dc[start : start + size, lanes]
            s = jnp.where(valid, mm(qb, kb, NT) * scale, MASKED)
            probs = jnp.exp(s - lse[start : start + size, head : head + 1])
            dp = mm(db, vb, NT)
            delta = jnp.sum(probs * dp, axis=-1, keepdims=True)
            ds = (probs * (dp - delta) * scale).astype(jnp.bfloat16)
            dq_parts.append(mm(ds, kb, NN))
            dk_parts.append(mm(ds, qb, TN))
            dv_parts.append(mm(probs.astype(jnp.bfloat16), db, TN))
        dq_rows.append(jnp.concatenate(dq_parts, axis=1))
        pads = ((start, extent - start - span), (0, 0))
        for parts, which in ((dk_parts, 0), (dv_parts, 1)):
            block = jnp.concatenate(parts, axis=1)
            rows = []
            if pads[0][0]:
                rows.append(jnp.zeros((pads[0][0], width), jnp.float32))
            rows.append(block)
            if pads[0][1]:
                rows.append(jnp.zeros((pads[0][1], width), jnp.float32))
            block = jnp.concatenate(rows, axis=0) if len(rows) > 1 else block
            if which == 0:
                dk = dk + block
            else:
                dv = dv + block
    cos, sin = cos_ref[...], sin_ref[...]
    dq = jnp.concatenate(dq_rows, axis=0)
    inner = slice(REACH, REACH + tokens)
    dq = (dq * cos[inner] + turn(dq * sin[inner], 1)).astype(jnp.bfloat16)
    dk = (dk * cos + turn(dk * sin, 1)).astype(jnp.bfloat16)
    dv = dv.astype(jnp.bfloat16)
    a = a_ref[...]
    spread(order, dps, dw_ref, 0, mm(dq, a[inner], TN))
    spread(order, dps, dw_ref, 1, mm(dk, a, TN))
    spread(order, dps, dw_ref, 2, mm(dv, a, TN))
    da_ref[...] += mm(dk, wide(order, dps, w_ref, 1), NN) + mm(dv, wide(order, dps, w_ref, 2), NN)
    da_ref[inner, :] += mm(dq, wide(order, dps, w_ref, 0), NN)

    @pl.when(step == pl.num_programs(0) - 1)
    def _():
        gg_ref[...] = jnp.sum(da_ref[...] * n_ref[...], axis=0, keepdims=True)


def feed_kernel(order, dps, y_ref, gain_ref, up_ref, w_ref, out0_ref, da0_ref,
                dw_ref, out_ref, da_ref, a_ref, u_ref):
    step = pl.program_id(0)

    @pl.when(step == 0)
    def _():
        normed, _ = norm_rows(y_ref[...])
        a_ref[...] = (normed * gain_ref[...].astype(jnp.float32)).astype(jnp.bfloat16)
        u_ref[...] = up_ref[...].astype(jnp.bfloat16)
        out_ref[...] = out0_ref[...]
        da_ref[...] = da0_ref[...]

    a, up = a_ref[...], u_ref[...]
    w0, w1, c = wide(order, dps, w_ref, 0), wide(order, dps, w_ref, 1), wide(order, dps, w_ref, 2)
    u0 = mm(w0, a, NT)
    u1 = mm(w1, a, NT)
    cdf = 0.5 * (1.0 + lax.erf(u0 * ROOT_HALF))
    activated = u0 * cdf
    slope = cdf + u0 * DENSITY * jnp.exp(-0.5 * u0 * u0)
    hidden = (activated * u1).astype(jnp.bfloat16)
    out_ref[...] += mm(hidden, c, TN)
    spread(order, dps, dw_ref, 2, mm(hidden, up, NN))
    dg = mm(c, up, NT)
    du0 = (dg * u1 * slope).astype(jnp.bfloat16)
    du1 = (dg * activated).astype(jnp.bfloat16)
    spread(order, dps, dw_ref, 0, mm(du0, a, NN))
    spread(order, dps, dw_ref, 1, mm(du1, a, NN))
    da_ref[...] += mm(du0, w0, TN) + mm(du1, w1, TN)


def full_spec(shape):
    return pl.BlockSpec(shape, lambda t: (0,) * len(shape))


def weight_spec(order, block):
    lead = tuple(2 if axis == "dp" else 1 for axis, _ in order)

    def place(t):
        return tuple(0 if axis == "dp" else (t // 2**j) % 2 for axis, j in order) + (0,) * len(block)

    return pl.BlockSpec(lead + block, place)


def lead_spec(shape):
    return pl.BlockSpec((1,) + shape[1:], lambda t: (t,) + (0,) * (len(shape) - 1))


def params():
    return pltpu.CompilerParams(
        dimension_semantics=("arbitrary",), vmem_limit_bytes=56 * 1024 * 1024
    )


def shaped(shape, dtype):
    return jax.ShapeDtypeStruct(shape, dtype)


def cost(flops, moved):
    return pl.CostEstimate(flops=int(flops), bytes_accessed=int(moved), transcendentals=0)


def body(
    dps,
    tensors,
    block_input,
    segment_ids,
    positions,
    attention_gain,
    feedforward_gain,
    qkv_weight,
    output_weight,
    expand_weight,
    contract_weight,
    cotangent,
):
    tokens, width = block_input.shape[1:]
    rows = qkv_weight.shape[0]
    hw = qkv_weight.shape[2]
    units = contract_weight.shape[0]
    heads = hw // HD
    extent = tokens + 2 * REACH
    f32, bf16 = jnp.float32, jnp.bfloat16

    x = block_input[0]
    upstream = cotangent[0]
    place = lax.axis_index("tensor")
    ahead = [(i, i + 1) for i in range(tensors - 1)]
    behind = [(i + 1, i) for i in range(tensors - 1)]
    before = lax.ppermute(x[tokens - REACH :], "tensor", ahead)
    after = lax.ppermute(x[:REACH], "tensor", behind)
    x_ext = jnp.concatenate([before, x, after], axis=0)

    orders = plans(dps, tensors)
    group = dps * tensors
    bits = len(orders[0])
    split = (2,) * bits
    gains = jnp.pad(jnp.stack([attention_gain, feedforward_gain]), ((0, GAIN_ROWS - 2), (0, 0)))
    first = jnp.concatenate(
        [jnp.transpose(qkv_weight, (1, 2, 0)), output_weight[None]], axis=0
    )
    stacked = jnp.concatenate(
        [jnp.transpose(expand_weight, (1, 2, 0)), contract_weight[None]], axis=0
    )
    cut = -(-units // (8 * CHUNKS)) * 8
    edges = [min(i * cut, units) for i in range(CHUNKS + 1)]
    shards = [first] + [stacked[:, lo:hi] for lo, hi in zip(edges[:-1], edges[1:])] + [gains]
    got_first, *got_feed, got_gains = gather_all(orders, dps, tensors, shards)
    w_attn = got_first.reshape(split + first.shape)
    at_zero = jnp.stack(
        [got_gains.reshape(split + gains.shape)[at_block(orders[3], d)] for d in range(dps)]
    )
    gain_one = at_zero[:, 0].reshape(1, width)
    gain_two = at_zero[:, 1].reshape(1, width)

    seg_all = jnp.pad(segment_ids[0], (REACH, REACH), constant_values=-1)
    pos_all = jnp.pad(positions[0], (REACH, REACH))
    seg_k = lax.dynamic_slice_in_dim(seg_all, place * tokens, extent, 0)
    pos = lax.dynamic_slice_in_dim(pos_all, place * tokens, extent, 0)
    seg_q = seg_k[REACH : REACH + tokens]
    half = HD // 2
    frequency = jnp.exp(jnp.arange(half, dtype=f32) * (-2.0 * math.log(10000.0) / HD))
    angles = pos.astype(f32)[:, None] * frequency[None, :]
    cos = jnp.tile(jnp.cos(angles), (1, 2 * heads))
    sin = jnp.tile(jnp.sin(angles), (1, 2 * heads))
    seg_q, seg_k = seg_q[:, None], seg_k[None, :]

    w_block = first.shape
    side = [
        full_spec((extent, width)),
        full_spec((1, width)),
        weight_spec(orders[0], w_block),
        full_spec((extent, hw)),
        full_spec((extent, hw)),
        full_spec((tokens, 1)),
        full_spec((1, extent)),
    ]
    qkv_shape = (tensors, 3, extent, hw)
    ctx_shape = (tensors, tokens, hw)
    lse_shape = (tensors, tokens, heads)
    attn_flops = 2 * tensors * extent * 4 * hw * width
    attn_bytes = 2 * 4 * width * width
    y, qkv, ctx, lse = pl.pallas_call(
        functools.partial(attend_kernel, orders[0], dps),
        grid=(tensors,),
        in_specs=side,
        out_specs=[
            full_spec((tokens, width)),
            lead_spec(qkv_shape),
            lead_spec(ctx_shape),
            lead_spec(lse_shape),
        ],
        out_shape=[
            shaped((tokens, width), f32),
            shaped(qkv_shape, bf16),
            shaped(ctx_shape, bf16),
            shaped(lse_shape, f32),
        ],
        scratch_shapes=[pltpu.VMEM((extent, width), bf16)],
        compiler_params=params(),
        cost_estimate=cost(attn_flops, attn_bytes),
        name="attend",
    )(x_ext, gain_one, w_attn, cos, sin, seg_q, seg_k)

    out, da_two = y, jnp.zeros((tokens, width), f32)
    feed_grads = []
    for order, got in zip(orders[1:], got_feed):
        block = got.shape[1:]
        size = block[1]
        got = got.reshape(split + block)
        dw, out, da_two = pl.pallas_call(
            functools.partial(feed_kernel, order, dps),
            grid=(tensors,),
            in_specs=[
                full_spec((tokens, width)),
                full_spec((1, width)),
                full_spec((tokens, width)),
                weight_spec(order, block),
                full_spec((tokens, width)),
                full_spec((tokens, width)),
            ],
            out_specs=[
                weight_spec(order, block),
                full_spec((tokens, width)),
                full_spec((tokens, width)),
            ],
            out_shape=[
                shaped(got.shape, bf16),
                shaped((tokens, width), f32),
                shaped((tokens, width), f32),
            ],
            scratch_shapes=[
                pltpu.VMEM((tokens, width), bf16),
                pltpu.VMEM((tokens, width), bf16),
            ],
            compiler_params=params(),
            cost_estimate=cost(18 * tensors * tokens * size * width, 12 * tensors * size * width),
            name="feed",
        )(y, gain_two, upstream, got, out, da_two)
        feed_grads.append(dw.reshape((group,) + block))

    normed_two, inverse_two = norm_rows(y)
    gain_grad_two = jnp.sum(da_two * normed_two, axis=0)
    grad_mid = upstream + norm_back(da_two, normed_two, inverse_two, gain_two.astype(f32))

    dw_attn, da_one, gain_grad_one = pl.pallas_call(
        functools.partial(attend_back_kernel, orders[0], dps),
        grid=(tensors,),
        in_specs=side
        + [
            lead_spec(qkv_shape),
            lead_spec(ctx_shape),
            lead_spec(lse_shape),
            full_spec((tokens, width)),
        ],
        out_specs=[
            weight_spec(orders[0], w_block),
            full_spec((extent, width)),
            full_spec((1, width)),
        ],
        out_shape=[
            shaped(split + w_block, bf16),
            shaped((extent, width), f32),
            shaped((1, width), f32),
        ],
        scratch_shapes=[
            pltpu.VMEM((extent, width), bf16),
            pltpu.VMEM((extent, width), f32),
            pltpu.VMEM((tokens, width), bf16),
        ],
        compiler_params=params(),
        cost_estimate=cost(2 * attn_flops, 2 * attn_bytes),
        name="attend_back",
    )(x_ext, gain_one, w_attn, cos, sin, seg_q, seg_k, qkv, ctx, lse, grad_mid)

    gain_grads = jnp.stack([gain_grad_one[0], gain_grad_two]).reshape(2, dps, rows)
    gain_block = jnp.pad(jnp.transpose(gain_grads, (1, 0, 2)), ((0, 0), (0, 6), (0, 0)))
    gain_block = gain_block.reshape(
        tuple(2 for _ in range(dps.bit_length() - 1)) + (1,) * (tensors.bit_length() - 1) + (8, rows)
    )
    names = [("dp", j) for j in range(dps.bit_length() - 2, -1, -1)]
    names += [("tensor", j) for j in range(tensors.bit_length() - 2, -1, -1)]
    spots = [names.index(bit) for bit in orders[3]]
    gain_block = jnp.broadcast_to(
        jnp.transpose(gain_block, spots + [bits, bits + 1]), split + (8, rows)
    ).reshape(group, 8, rows)
    owned, *owned_feed, owned_gains = scatter_all(
        orders, dps, tensors, [dw_attn.reshape((group,) + w_block)] + feed_grads + [gain_block]
    )

    to_before = lax.ppermute(da_one[:REACH].astype(bf16), "tensor", behind).astype(f32)
    to_after = lax.ppermute(da_one[tokens + REACH :].astype(bf16), "tensor", ahead).astype(f32)
    da_total = da_one[REACH : REACH + tokens]
    da_total = da_total + jnp.concatenate(
        [to_after, jnp.zeros((tokens - 2 * REACH, width), f32), to_before], axis=0
    )
    normed_one, inverse_one = norm_rows(x)
    input_grad = grad_mid + norm_back(da_total, normed_one, inverse_one, gain_one.astype(f32))

    feed = jnp.concatenate(owned_feed, axis=1)
    return (
        out[None],
        input_grad[None],
        owned_gains[0],
        owned_gains[1],
        jnp.transpose(owned[:3], (2, 0, 1)),
        owned[3],
        jnp.transpose(feed[:2], (2, 0, 1)),
        feed[2],
    )


def solution(mesh):
    return jax.shard_map(
        functools.partial(body, mesh.shape["dp"], mesh.shape["tensor"]),
        mesh=mesh,
        in_specs=(
            P("dp", "tensor", None),
            P("dp", None),
            P("dp", None),
            P("dp"),
            P("dp"),
            P("dp", None, "tensor"),
            P("tensor", "dp"),
            P("dp", None, "tensor"),
            P("tensor", "dp"),
            P("dp", "tensor", None),
        ),
        out_specs=(
            P("dp", "tensor", None),
            P("dp", "tensor", None),
            P("dp"),
            P("dp"),
            P("dp", None, "tensor"),
            P("tensor", "dp"),
            P("dp", None, "tensor"),
            P("tensor", "dp"),
        ),
        check_vma=False,
    )
```
